32 devices in a mesh: dp: 2 (over x), expert: 16 (over z, y, core).
Axes of the slice: x: 2, y: 2, z: 4, core: 2. Of those that a mesh axis runs over, the one named last changes fastest.
Arguments:
- tokens: bfloat16 [4096, 2048], P(('dp', 'expert')), may hold values from -6 to 6
- expert_ids: int32 [4096, 4], P(('dp', 'expert')), may hold values from 0 to 31, all different within a row; in each aligned block of 128 rows (0 to 127, 128 to 255, ...) at most 28 rows name the same one
- gate_weights: float32 [4096, 4], P(('dp', 'expert')), may hold values from 0.05 to 0.5
- slot_of_expert: int32 [32], replicated, may hold values from 0 to 31, each once
- w_gate: bfloat16 [32, 2048, 768], P('expert'), may hold values from -0.125 to 0.125
- w_up: bfloat16 [32, 2048, 768], P('expert'), may hold values from -0.125 to 0.125
- w_down: bfloat16 [32, 768, 2048], P('expert'), may hold values from -0.21875 to 0.21875
- d_out: bfloat16 [4096, 2048], P(('dp', 'expert')), may hold values from -6 to 6
Outputs:
- layer_out: bfloat16 [4096, 2048], P(('dp', 'expert'))
- d_tokens: bfloat16 [4096, 2048], P(('dp', 'expert'))
- d_gates: float32 [4096, 4], P(('dp', 'expert'))
- grad_gate: bfloat16 [32, 2048, 768], P('expert', 'dp')
- grad_up: bfloat16 [32, 2048, 768], P('expert', 'dp')
- grad_down: bfloat16 [32, 768, 2048], P('expert', None, 'dp')
The draws below stay inside these ranges and needn't reach their ends.
Inputs may be any that keep to these rules, and one draw needn't show every extreme that they name: `expert_ids`: each row names 4 different experts. Among the 128 rows of one device (aligned blocks of rows) no expert is named more than 28 times, and in every draw some expert is named exactly 28 times in some block. A permutation: expert e's weights stand at index slot_of_expert[e] of w_gate, w_up and w_down, and its gradients at that index of the outputs.
All inputs are finite; a program needn't handle non-finite values.
Results may differ from the reference program's by a relative error of at most 0.0095.
Values may be sent and summed in bfloat16 or wider, within the bound.
No kernel may reach another device: no remote copies, remote signals or barrier semaphores. Data moves between devices by JAX's collectives and lax.ppermute only.
A program may use at most 192 MiB of HBM per device.

```python
import math
import jax
import jax.numpy as jnp
import numpy as np
from jax import lax

D = 2048
FF = 768
TOP = 4
TOK_DEV = 128
EXPERTS = 32
CAP = 28
TOKENS = 4096
N_DP = 2
N_EXPERT = 16


def block_scale(stream_key, shape, cuts, smallest, top_value):
    factor_of = 1.0
    for position, parts in cuts:
        draws = jax.random.uniform(jax.random.fold_in(jax.random.fold_in(stream_key, 6), position), (parts,), jnp.float32, smallest / len(cuts), top_value / len(cuts))
        factor_of = factor_of * jnp.repeat(jnp.exp(draws), shape[position] // parts).reshape((-1,) + (1,) * (len(shape) - 1 - position))
    return factor_of


def assign_block(rng, own, number, rows, amount, top, bound, lean):
    sequence = jax.random.permutation(rng, amount)
    packed, ordinary = load_shares(amount, rows * top, bound, lean, True), load_shares(amount, rows * top, bound, lean, False)
    places = jnp.arange(amount)

    def named(tallies, turn):
        used = int((tallies > 0).sum())
        fixed = max(1, used // 4)
        passed = fixed + (places - fixed + turn * (used - fixed)) % max(1, amount - fixed)
        return jnp.zeros((amount,), jnp.int32).at[sequence[jnp.where(places < fixed, places, passed)]].set(jnp.asarray(tallies, jnp.int32))

    tallies = jnp.where(number % 4 == 0, named(packed, number // 4), named(ordinary, number - number // 4 - 1))
    mixed = jax.random.permutation(jax.random.fold_in(own, 3), amount)
    donor, sink = mixed[0:amount // 2 * 2:2], mixed[1:amount // 2 * 2:2]
    margin = jnp.minimum(tallies[donor] - 1, bound - tallies[sink]) // 2
    margin = jnp.where((donor == sequence[0]) | (sink == sequence[0]) | (tallies[sink] == 0), 0, jnp.maximum(margin, 0))
    passed = jax.random.randint(jax.random.fold_in(own, 4), (amount // 2,), 0, 1 << 20) % (margin + 1)
    tallies = tallies.at[donor].add(-passed).at[sink].add(passed)
    labels = jnp.searchsorted(jnp.cumsum(tallies), jnp.arange(rows * top), side="right").astype(jnp.int32)
    grid = labels.reshape(top, rows).T
    grid = grid[jax.random.permutation(jax.random.fold_in(own, 1), rows)]
    turn = jax.random.randint(jax.random.fold_in(own, 2), (rows, 1), 0, top)
    return jnp.take_along_axis(grid, (jnp.arange(top)[None, :] + turn) % top, axis=1)


def load_shares(count, total, reach, lean, full):
    portions = [(1 << 20) // math.isqrt(rank ** lean) + 1 for rank in range(1, count + 1)]
    largest = reach if full else min(reach, max(-(-total // count), total * portions[0] // sum(portions)))
    least = 1 if total - largest >= count - 1 else 0
    given, spare = [largest] + [least] * (count - 1), total - largest - least * (count - 1)
    while spare > 0:
        free = [i for i in range(1, count) if given[i] < largest] or [i for i in range(1, count) if given[i] < reach]
        whole, left = sum([portions[i] for i in free]), spare
        for i in free:
            extra = min(reach - given[i], max(1, left * portions[i] // whole), spare)
            given[i] = given[i] + extra
            spare = spare - extra
    return np.array(given)


def scatter_about(key, shape, width, bound, shards=(), held_as=jnp.bfloat16):
    level = block_scale(key, shape, shards, -0.22, 0.18) if shards else 1.0
    entries = jax.random.normal(key, shape, jnp.float32) * width * level
    return jnp.minimum(jnp.maximum(entries, -bound), bound).astype(held_as)


def setup_inputs(seed: int = 0) -> dict:
    keys = jax.random.split(jax.random.key(seed), 9)
    tokens = scatter_about(keys[0], (TOKENS, D), 1.0, 6.0, ((0, 32),))
    expert_ids_keys = jax.random.split(jax.random.fold_in(keys[1], 1), TOKENS // TOK_DEV)
    expert_ids_turns = jax.random.permutation(jax.random.fold_in(keys[1], 3), TOKENS // TOK_DEV)
    expert_ids = jax.vmap(lambda own, number: assign_block(jax.random.fold_in(keys[1], 2), own, number, TOK_DEV, EXPERTS, TOP, CAP, 2))(expert_ids_keys, expert_ids_turns).reshape((TOKENS, TOP))
    gate_weights = jnp.clip(0.05 + 0.45 * jax.random.uniform(keys[2], (TOKENS, TOP), jnp.float32) ** block_scale(keys[2], (TOKENS, TOP), ((0, 32),), -0.2, 0.2), 0.05, 0.5)
    slot_of_expert = jax.random.permutation(keys[3], EXPERTS).astype(jnp.int32)
    w_gate = scatter_about(keys[4], (EXPERTS, D, FF), D ** -0.5, 0.125, ((0, 16),))
    w_up = scatter_about(keys[5], (EXPERTS, D, FF), D ** -0.5, 0.125, ((0, 16),))
    w_down = scatter_about(keys[6], (EXPERTS, FF, D), FF ** -0.5, 0.21875, ((0, 16),))
    d_out = scatter_about(keys[7], (TOKENS, D), 1.0, 6.0, ((0, 32),))
    return dict(tokens=tokens, expert_ids=expert_ids, gate_weights=gate_weights, slot_of_expert=slot_of_expert, w_gate=w_gate, w_up=w_up, w_down=w_down, d_out=d_out)


def take_rows(source_rows, row_ids):
    return source_rows[row_ids]


def reference(tokens, expert_ids, gate_weights, slot_of_expert, w_gate, w_up, w_down, d_out):
    per_group = TOK_DEV * N_EXPERT
    count = per_group * TOP
    most_rows = CAP * N_EXPERT
    slots = slot_of_expert[expert_ids].astype(jnp.int32).reshape(N_DP, count)
    expert_range = jnp.arange(EXPERTS, dtype=jnp.int32)
    onehot = (slots[:, :, None] == expert_range).astype(jnp.int32)
    ranks = jnp.sum((jnp.cumsum(onehot, axis=1) - 1) * onehot, axis=2).astype(jnp.int32)
    group_rows = jnp.broadcast_to(jnp.arange(N_DP, dtype=jnp.int32)[:, None], (N_DP, count))
    assign_ids = jnp.broadcast_to(jnp.arange(count, dtype=jnp.int32)[None, :], (N_DP, count))
    table_ids = jnp.full((N_DP, EXPERTS, most_rows), count, jnp.int32)
    table_ids = table_ids.at[group_rows, slots, ranks].set(assign_ids)
    zero_row = jnp.zeros((N_DP, 1, D), jnp.bfloat16)
    tok_padded = jnp.concatenate([tokens.reshape(N_DP, per_group, D), zero_row], axis=1)
    d_routed = (gate_weights[:, :, None] * d_out[:, None, :].astype(jnp.float32)).astype(jnp.bfloat16)
    dy_padded = jnp.concatenate([d_routed.reshape(N_DP, count, D), zero_row], axis=1)

    def per_slot(slot_index):
        assign = lax.dynamic_index_in_dim(table_ids, slot_index, 1, keepdims=False)
        owners = (assign // TOP).astype(jnp.int32)
        inputs = jax.vmap(take_rows)(tok_padded, owners).astype(jnp.float32)
        d_rows = jax.vmap(take_rows)(dy_padded, assign).astype(jnp.float32)
        gate_mat = lax.dynamic_index_in_dim(w_gate, slot_index, 0, keepdims=False).astype(jnp.float32)
        up_mat = lax.dynamic_index_in_dim(w_up, slot_index, 0, keepdims=False).astype(jnp.float32)
        down_mat = lax.dynamic_index_in_dim(w_down, slot_index, 0, keepdims=False).astype(jnp.float32)
        pre_gate = jnp.einsum("rcd,df->rcf", inputs, gate_mat)
        pre_up = jnp.einsum("rcd,df->rcf", inputs, up_mat)
        sigma = jax.nn.sigmoid(pre_gate)
        silu_gate = pre_gate * sigma
        hidden = (silu_gate * pre_up).astype(jnp.bfloat16)
        outputs = jnp.einsum("rcf,fd->rcd", hidden.astype(jnp.float32), down_mat).astype(jnp.bfloat16)
        d_hidden = jnp.einsum("rcd,fd->rcf", d_rows, down_mat)
        d_gate_pre = (d_hidden * pre_up * sigma * (1.0 + pre_gate * (1.0 - sigma))).astype(jnp.bfloat16)
        d_up_pre = (d_hidden * silu_gate).astype(jnp.bfloat16)
        d_inputs = jnp.einsum("rcf,df->rcd", d_gate_pre.astype(jnp.float32), gate_mat)
        d_inputs = d_inputs + jnp.einsum("rcf,df->rcd", d_up_pre.astype(jnp.float32), up_mat)
        d_inputs = d_inputs.astype(jnp.bfloat16)
        part_gate = jnp.einsum("rcd,rcf->rdf", inputs, d_gate_pre.astype(jnp.float32))
        part_up = jnp.einsum("rcd,rcf->rdf", inputs, d_up_pre.astype(jnp.float32))
        part_down = jnp.einsum("rcf,rcd->rfd", hidden.astype(jnp.float32), d_rows)
        part_gate = lax.optimization_barrier(part_gate.astype(jnp.bfloat16)).astype(jnp.float32)
        part_up = lax.optimization_barrier(part_up.astype(jnp.bfloat16)).astype(jnp.float32)
        part_down = lax.optimization_barrier(part_down.astype(jnp.bfloat16)).astype(jnp.float32)
        return (outputs, d_inputs, jnp.sum(part_gate, axis=0).astype(jnp.bfloat16),
                jnp.sum(part_up, axis=0).astype(jnp.bfloat16), jnp.sum(part_down, axis=0).astype(jnp.bfloat16))

    outs_all, d_in_all, grad_gate, grad_up, grad_down = lax.map(per_slot, expert_range)
    expert_out = outs_all[slots, group_rows, ranks].reshape(N_DP * per_group, TOP, D).astype(jnp.float32)
    d_routed_in = d_in_all[slots, group_rows, ranks].reshape(N_DP * per_group, TOP, D).astype(jnp.float32)
    layer_out = jnp.sum(gate_weights[:, :, None] * expert_out, axis=1).astype(jnp.bfloat16)
    d_gates = jnp.sum(d_out[:, None, :].astype(jnp.float32) * expert_out, axis=2)
    d_tokens = jnp.sum(d_routed_in, axis=1).astype(jnp.bfloat16)
    return (layer_out, d_tokens, d_gates, grad_gate, grad_up, grad_down)
```

```python
import jax
import jax.numpy as jnp
import numpy as np
from jax import lax
from jax.experimental import pallas as pl
from jax.experimental.pallas import tpu as pltpu
from jax.sharding import PartitionSpec as P

BF = jnp.bfloat16
F32 = jnp.float32
TAG = 128
HALF = 64
LAST = (((1,), (1,)), ((), ()))
FIRST = (((0,), (0,)), ((), ()))


def ring_of(chips):
    z_len = 4 if chips % 8 == 0 else chips
    y_len = chips // z_len
    if y_len == 1:
        return list(range(z_len))
    cells = []
    for y in range(y_len):
        zs = range(1, z_len) if y % 2 == 0 else range(z_len - 1, 0, -1)
        cells += [(z, y) for z in zs]
    cells += [(0, y) for y in range(y_len - 1, -1, -1)]
    return [z * y_len + y for z, y in cells]


class Ring:
    def __init__(self, peers):
        self.chips = m = peers // 2
        order = ring_of(m)
        self.fwd = [(2 * order[i] + c, 2 * order[(i + 1) % m] + c) for i in range(m) for c in (0, 1)]
        self.bwd = [(b, a) for a, b in self.fwd]
        self.core = [(i, i ^ 1) for i in range(peers)]

    def steps(self, long_fwd):
        n_fwd = self.chips // 2 if long_fwd else (self.chips - 1) // 2
        return n_fwd, self.chips - 1 - n_fwd

    def gather(self, own, long_fwd):
        n_fwd, n_bwd = self.steps(long_fwd)
        held = [None] * self.chips
        held[0] = ahead = back = own
        for k in range(1, max(n_fwd, n_bwd) + 1):
            if k <= n_fwd:
                held[k] = ahead = lax.ppermute(ahead, "expert", self.fwd)
            if k <= n_bwd:
                held[self.chips - k] = back = lax.ppermute(back, "expert", self.bwd)
        return held

    def scatter(self, part, long_fwd):
        m = self.chips
        n_fwd, n_bwd = self.steps(long_fwd)
        ahead, back = part((m - n_fwd) % m), part(n_bwd)
        total = part(0).astype(F32)
        for k in range(1, max(n_fwd, n_bwd) + 1):
            if k <= n_fwd:
                got = lax.ppermute(ahead, "expert", self.fwd).astype(F32)
                left = n_fwd - k
                if left:
                    ahead = (got + part(m - left).astype(F32)).astype(BF)
                else:
                    total = total + got
            if k <= n_bwd:
                got = lax.ppermute(back, "expert", self.bwd).astype(F32)
                left = n_bwd - k
                if left:
                    back = (got + part(left).astype(F32)).astype(BF)
                else:
                    total = total + got
        return total


def column_blocks(width, size=512):
    return [(a, min(size, width - a)) for a in range(0, width, size)]


def build_onehot(lanes_ref, tags):
    slot_of = lanes_ref[0:1, :]
    place_of = lanes_ref[1:2, :]
    chunk_of = lanes_ref[2:3, :]
    rows = tags[0].shape[0]
    earlier = lax.broadcasted_iota(jnp.int32, (rows, rows), 1) < lax.broadcasted_iota(
        jnp.int32, (rows, rows), 0
    )
    earlier = jnp.where(earlier, 1.0, 0.0).astype(BF)
    blocks = []
    for j, tag in enumerate(tags):
        tag = tag.astype(F32)
        named = tag[:, 0:1] == slot_of
        for k in range(1, 4):
            named = named | (tag[:, k:k + 1] == slot_of)
        named = jnp.where(named, 1.0, 0.0)
        rank = jnp.dot(earlier, named.astype(BF), preferred_element_type=F32)
        keep = jnp.where((rank == place_of) & (chunk_of == float(j)), named, 0.0)
        blocks.append(keep.astype(BF))
    return blocks


def place_rows(blocks, chunks, width, mine_ref, theirs_ref):
    local, spots = mine_ref.shape[0], mine_ref.shape[1]
    for a, size in column_blocks(width):
        rows = None
        for block, chunk in zip(blocks, chunks):
            term = lax.dot_general(block, chunk[:, a:a + size], FIRST, preferred_element_type=F32)
            rows = term if rows is None else rows + term
        rows = rows.astype(BF).reshape(2 * local, spots, size)
        mine_ref[:, :, a:a + size] = rows[:local]
        theirs_ref[:, :, a:a + size] = rows[local:]


def vmem(n):
    return [pl.BlockSpec(memory_space=pltpu.VMEM)] * n


def dispatch_tagged(lanes, chunks, width, local, spots, dp, n_dp, far, want_onehot):
    rows = chunks[0].shape[0]
    count = len(chunks)
    full = chunks[0].shape[1]
    out_width = full if far else width
    shapes = [jax.ShapeDtypeStruct((local, spots, out_width), BF)] * 2
    if want_onehot:
        shapes.append(jax.ShapeDtypeStruct((count * rows, lanes.shape[1]), BF))
    if far:
        shapes += [jax.ShapeDtypeStruct((local, spots, width // n_dp), BF)] * (2 * (n_dp - 1))

    def body(dp_ref, lanes_ref, *refs):
        ins, outs = refs[:count], refs[count:]
        blocks = build_onehot(lanes_ref, [c[:, width:width + TAG] for c in ins])
        if want_onehot:
            for j, block in enumerate(blocks):
                outs[2][j * rows:(j + 1) * rows, :] = block
        place_rows(blocks, ins, out_width, outs[0], outs[1])
        if far:
            size = width // n_dp
            for j in range(1, n_dp):
                start = pl.multiple_of(lax.rem(dp_ref[0] + j, n_dp) * size, size)
                for side in (0, 1):
                    out = outs[2 + int(want_onehot) + 2 * (j - 1) + side]
                    out[...] = outs[side][:, :, pl.ds(start, size)]

    return pl.pallas_call(
        body,
        in_specs=[pl.BlockSpec(memory_space=pltpu.SMEM)] + vmem(1 + count),
        out_specs=vmem(len(shapes)),
        out_shape=shapes,
    )(dp, lanes, *chunks)


def dispatch_plain(onehot_t, chunks, local, spots):
    rows, width = chunks[0].shape
    count = len(chunks)

    def body(oh_ref, *refs):
        ins, outs = refs[:count], refs[count:]
        blocks = [oh_ref[j * rows:(j + 1) * rows, :] for j in range(count)]
        place_rows(blocks, ins, width, outs[0], outs[1])

    return pl.pallas_call(
        body,
        in_specs=vmem(1 + count),
        out_specs=vmem(2),
        out_shape=[jax.ShapeDtypeStruct((local, spots, width), BF)] * 2,
    )(onehot_t, *chunks)


def combine(onehot_t, parts, index, spots):
    toks = onehot_t.shape[0]
    width = parts[0].shape[1]
    count = len(parts)

    def body(oh_ref, *refs):
        rows = jnp.concatenate([r[...] for r in refs[:count]], axis=0)
        refs[count][...] = jnp.dot(oh_ref[...], rows, preferred_element_type=F32).astype(BF)

    step = toks // 4
    return pl.pallas_call(
        body,
        grid=(4,),
        in_specs=[pl.BlockSpec((step, onehot_t.shape[1]), lambda i: (i, 0))]
        + [pl.BlockSpec((spots, width), lambda i: (index, 0))] * count,
        out_specs=pl.BlockSpec((step, width), lambda i: (i, 0)),
        out_shape=jax.ShapeDtypeStruct((toks, width), BF),
    )(onehot_t, *parts)


def forward(slot, s, pieces, wg, wu, wd, block, width):
    spots = pieces[0].shape[1]
    full = pieces[0].shape[2]
    count = len(pieces)
    most = count * spots
    half = most // 2
    ff = wg.shape[2]

    def body(slot_ref, *refs):
        ins = refs[:count]
        wg_ref, wu_ref, wd_ref = refs[count:count + 3]
        pg_ref, pu_ref, hs_ref, meta_ref, near_ref, away_ref, x_ref, acc_ref = refs[count + 3:]
        f = pl.program_id(0)

        @pl.when(f == 0)
        def _():
            for i in range(count):
                x_ref[i * spots:(i + 1) * spots, :] = ins[i][0, :, :width]
                tag = ins[i][0, :, width:width + TAG].astype(F32)
                lane = lax.broadcasted_iota(jnp.int32, tag.shape, 1)
                match = (tag == slot_ref[0].astype(F32)) & (lane < 12)
                gates = pltpu.roll(tag, HALF, axis=1)
                gate = jnp.sum(jnp.where(match, gates, 0.0), axis=1, keepdims=True)
                meta = jnp.where(match, 1.0, 0.0) + jnp.where(lane == HALF, gate, 0.0)
                meta_ref[i * spots:(i + 1) * spots, :] = meta

        x = x_ref[...]
        gate = meta_ref[:, HALF:HALF + 1]
        pg = jnp.dot(x, wg_ref[0], preferred_element_type=F32)
        pu = jnp.dot(x, wu_ref[0], preferred_element_type=F32)
        pg_ref[...] = pg
        pu_ref[...] = pu
        hidden = pg * (1.0 / (1.0 + jnp.exp(-pg))) * pu
        hs_ref[...] = (gate * hidden).astype(BF)
        part = jnp.dot(hidden.astype(BF), wd_ref[0], preferred_element_type=F32)

        @pl.when(f == 0)
        def _():
            acc_ref[...] = part

        @pl.when(f > 0)
        def _():
            acc_ref[...] += part

        @pl.when(f == pl.num_programs(0) - 1)
        def _():
            rows = (gate * acc_ref[...]).astype(BF)
            near_ref[...] = rows[:half]
            away_ref[...] = rows[half:]

    cols = pl.BlockSpec((most, block), lambda f: (0, f))
    whole = lambda shape: pl.BlockSpec(shape, lambda f: (0, 0))
    return pl.pallas_call(
        body,
        grid=(ff // block,),
        in_specs=[pl.BlockSpec(memory_space=pltpu.SMEM)]
        + [pl.BlockSpec((1, spots, full), lambda f: (s, 0, 0))] * count
        + [
            pl.BlockSpec((1, width, block), lambda f: (s, 0, f)),
            pl.BlockSpec((1, width, block), lambda f: (s, 0, f)),
            pl.BlockSpec((1, block, width), lambda f: (s, f, 0)),
        ],
        out_specs=[cols, cols, cols, whole((most, TAG)), whole((half, width)), whole((half, width))],
        out_shape=[
            jax.ShapeDtypeStruct((most, ff), F32),
            jax.ShapeDtypeStruct((most, ff), F32),
            jax.ShapeDtypeStruct((most, ff), BF),
            jax.ShapeDtypeStruct((most, TAG), F32),
            jax.ShapeDtypeStruct((half, width), BF),
            jax.ShapeDtypeStruct((half, width), BF),
        ],
        scratch_shapes=[pltpu.VMEM((most, width), BF), pltpu.VMEM((most, width), F32)],
    )(slot, *pieces, wg, wu, wd)


def backward(s, pieces, pg, pu, meta, wg, wu, wd, block):
    spots, width = pieces[0].shape[1:]
    count = len(pieces)
    most = count * spots
    half = most // 2
    ff = wg.shape[2]

    def body(*refs):
        ins = refs[:count]
        pg_ref, pu_ref, meta_ref, wg_ref, wu_ref, wd_ref = refs[count:count + 6]
        act_ref, near_ref, away_ref, g_ref, acc_ref, dot_ref = refs[count + 6:]
        f = pl.program_id(0)

        @pl.when(f == 0)
        def _():
            for i in range(count):
                g_ref[i * spots:(i + 1) * spots, :] = ins[i][0]

        gate = meta_ref[:, HALF:HALF + 1]
        raw = lax.dot_general(g_ref[...], wd_ref[0], LAST, preferred_element_type=F32)
        pg = pg_ref[...]
        pu = pu_ref[...]
        sigma = 1.0 / (1.0 + jnp.exp(-pg))
        silu = pg * sigma
        hidden = (silu * pu).astype(BF).astype(F32)
        row_dot = jnp.sum(hidden * raw, axis=1, keepdims=True)
        dh = gate * raw
        dgp = (dh * pu * sigma * (1.0 + pg * (1.0 - sigma))).astype(BF)
        dup = (dh * silu).astype(BF)
        act_ref[0] = dgp
        act_ref[1] = dup
        part = lax.dot_general(dgp, wg_ref[0], LAST, preferred_element_type=F32)
        part = part + lax.dot_general(dup, wu_ref[0], LAST, preferred_element_type=F32)

        @pl.when(f == 0)
        def _():
            acc_ref[...] = part
            dot_ref[...] = row_dot

        @pl.when(f > 0)
        def _():
            acc_ref[...] += part
            dot_ref[...] += row_dot

        @pl.when(f == pl.num_programs(0) - 1)
        def _():
            rows = acc_ref[...].astype(BF)
            lane = lax.broadcasted_iota(jnp.int32, (most, TAG), 1)
            value = jnp.broadcast_to(dot_ref[...], (most, TAG))
            high = value.astype(BF).astype(F32)
            middle = (value - high).astype(BF).astype(F32)
            low = value - high - middle
            piece = jnp.where(lane < 4, high, jnp.where(lane < 8, middle, low))
            tag = jnp.where((meta_ref[...] > 0.5) & (lane < 12), piece, 0.0).astype(BF)
            near_ref[:, :width] = rows[:half]
            near_ref[:, width:] = tag[:half]
            away_ref[:, :width] = rows[half:]
            away_ref[:, width:] = tag[half:]

    cols = pl.BlockSpec((most, block), lambda f: (0, f))
    whole = lambda shape: pl.BlockSpec(shape, lambda f: (0, 0))
    return pl.pallas_call(
        body,
        grid=(ff // block,),
        in_specs=[pl.BlockSpec((1, spots, width), lambda f: (s, 0, 0))] * count
        + [
            cols,
            cols,
            whole((most, TAG)),
            pl.BlockSpec((1, width, block), lambda f: (s, 0, f)),
            pl.BlockSpec((1, width, block), lambda f: (s, 0, f)),
            pl.BlockSpec((1, block, width), lambda f: (s, f, 0)),
        ],
        out_specs=[
            pl.BlockSpec((2, most, block), lambda f: (0, 0, f)),
            whole((half, width + TAG)),
            whole((half, width + TAG)),
        ],
        out_shape=[
            jax.ShapeDtypeStruct((2, most, ff), BF),
            jax.ShapeDtypeStruct((half, width + TAG), BF),
            jax.ShapeDtypeStruct((half, width + TAG), BF),
        ],
        scratch_shapes=[
            pltpu.VMEM((most, width), BF),
            pltpu.VMEM((most, width), F32),
            pltpu.VMEM((most, 1), F32),
        ],
    )(*pieces, pg, pu, meta, wg, wu, wd)


def in_grads(dp, pieces, far, acts):
    local, spots, _ = pieces[0].shape
    count = len(pieces)
    most = count * spots
    part = far[0][0].shape[2]
    sets = 1 + len(far)
    ff = acts[0][0].shape[2]
    steps = 2
    block = part // steps

    def body(dp_ref, *refs):
        xs = refs[:sets * count]
        sides = refs[sets * count:sets * (count + local)]
        outs = refs[sets * (count + local):sets * (count + local) + 2]
        x_ref = refs[-1]
        s = pl.program_id(0)
        for q in range(sets):
            for i in range(count):
                x_ref[q * most + i * spots:q * most + (i + 1) * spots, :] = xs[q * count + i][0]
        for which in (0, 1):
            for slot in range(local):
                @pl.when(s == slot)
                def _():
                    total = None
                    for q in range(sets):
                        term = lax.dot_general(
                            x_ref[q * most:(q + 1) * most, :], sides[q * local + slot][which],
                            FIRST, preferred_element_type=F32,
                        )
                        total = term if total is None else total + term
                    outs[which][0] = total.astype(BF)

    own = pl.BlockSpec((1, spots, block), lambda s, b, dp_ref: (s, 0, dp_ref[0] * steps + b))
    other = pl.BlockSpec((1, spots, block), lambda s, b, dp_ref: (s, 0, b))
    side = pl.BlockSpec((2, most, ff), lambda s, b, dp_ref: (0, 0, 0))
    out = pl.BlockSpec((1, block, ff), lambda s, b, dp_ref: (s, b, 0))
    return pl.pallas_call(
        body,
        grid_spec=pltpu.PrefetchScalarGridSpec(
            num_scalar_prefetch=1,
            grid=(local, steps),
            in_specs=[own] * count + [other] * (count * len(far)) + [side] * (sets * local),
            out_specs=[out] * 2,
            scratch_shapes=[pltpu.VMEM((sets * most, block), BF)],
        ),
        out_shape=[jax.ShapeDtypeStruct((local, part, ff), BF)] * 2,
    )(dp, *pieces, *[p for f in far for p in f], *[a for q in acts for a in q])


def down_grad(dp, pieces, far, hs):
    local, spots, width = pieces[0].shape
    count = len(pieces)
    most = count * spots
    sets = 1 + len(far)
    part = width // sets
    ff = hs[0][0].shape[1]
    steps = 2
    block = part // steps

    def body(dp_ref, *refs):
        xs = refs[:sets * count]
        sides = refs[sets * count:sets * (count + local)]
        out_ref = refs[sets * (count + local)]
        x_ref = refs[-1]
        s = pl.program_id(0)
        for q in range(sets):
            for i in range(count):
                x_ref[q * most + i * spots:q * most + (i + 1) * spots, :] = xs[q * count + i][0]
        for slot in range(local):
            @pl.when(s == slot)
            def _():
                total = None
                for q in range(sets):
                    term = lax.dot_general(
                        sides[q * local + slot][...], x_ref[q * most:(q + 1) * most, :],
                        FIRST, preferred_element_type=F32,
                    )
                    total = term if total is None else total + term
                out_ref[0] = total.astype(BF)

    own = pl.BlockSpec((1, spots, block), lambda s, b, dp_ref: (s, 0, dp_ref[0] * steps + b))
    other = pl.BlockSpec((1, spots, block), lambda s, b, dp_ref: (s, 0, b))
    side = pl.BlockSpec((most, ff), lambda s, b, dp_ref: (0, 0))
    return pl.pallas_call(
        body,
        grid_spec=pltpu.PrefetchScalarGridSpec(
            num_scalar_prefetch=1,
            grid=(local, steps),
            in_specs=[own] * count + [other] * (count * len(far)) + [side] * (sets * local),
            out_specs=pl.BlockSpec((1, ff, block), lambda s, b, dp_ref: (s, 0, b)),
            scratch_shapes=[pltpu.VMEM((sets * most, block), BF)],
        ),
        out_shape=jax.ShapeDtypeStruct((local, ff, part), BF),
    )(dp, *pieces, *[p for f in far for p in f], *[a for q in hs for a in q])


def pick(x, index, parts):
    size = x.shape[-1] // parts
    out = x[..., :size]
    for i in range(1, parts):
        out = jnp.where(index == i, x[..., i * size:(i + 1) * size], out)
    return out


def on_device(tokens, expert_ids, gate_weights, slot_of_expert, w_gate, w_up, w_down, d_out):
    peers = lax.axis_size("expert")
    n_dp = lax.axis_size("dp")
    me = lax.axis_index("expert")
    dp = lax.axis_index("dp")
    local = w_gate.shape[0]
    experts_all = local * peers
    rows_dev, width = tokens.shape
    top = expert_ids.shape[1]
    ff = w_gate.shape[2]
    block = 256 if ff % 256 == 0 else ff
    cap = rows_dev * top * 7 // (4 * experts_all)
    ring = Ring(peers)
    chips = ring.chips
    per = 1
    while (per * cap) % 16:
        per *= 2
    spots = per * cap
    arrival = sorted(range(chips), key=lambda d: min(d, chips - d))
    sets = [arrival[i:i + per] for i in range(0, chips, per)]

    expert_range = jnp.arange(experts_all, dtype=jnp.int32)
    slot_ids = jnp.sum(jnp.where(expert_ids[:, :, None] == expert_range, slot_of_expert, 0), axis=2)
    ids = slot_ids.astype(F32)
    high = lax.reduce_precision(gate_weights, 8, 7)
    middle = lax.reduce_precision(gate_weights - high, 8, 7)
    low = gate_weights - high - middle
    blank = jnp.zeros((rows_dev, HALF - 3 * top), F32)
    tag = jnp.concatenate([ids, ids, ids, blank, high, middle, low, blank], axis=1).astype(BF)

    def dp_shift(arr, j):
        return lax.ppermute(arr, "dp", [(i, (i + j) % n_dp) for i in range(n_dp)])

    def dp_shift_across(arr, j):
        pairs = [
            (i * peers + e, (i + j) % n_dp * peers + (e ^ 1)) for i in range(n_dp) for e in range(peers)
        ]
        return lax.ppermute(arr, ("dp", "expert"), pairs)

    def swap(arr):
        return lax.ppermute(arr, "expert", ring.core)

    far_own = jnp.concatenate(
        [
            dp_shift(jnp.concatenate([pick(d_out, (dp + j) % n_dp, n_dp), tag], axis=1), j)
            for j in range(1, n_dp)
        ],
        axis=1,
    )
    tok_chunks = ring.gather(jnp.concatenate([tokens, tag], axis=1), True)
    d_chunks = ring.gather(d_out, False)
    far_chunks = ring.gather(far_own, True)

    spot = np.arange(2 * local * spots)
    which = spot // spots
    own_base = (me * local).astype(F32)
    other_base = ((me ^ 1) * local).astype(F32)
    slot_lane = jnp.where(which < local, own_base + which, other_base + which - local)
    lanes = jnp.stack(
        [slot_lane, jnp.asarray(spot % cap, F32), jnp.asarray(spot % spots // cap, F32)]
        + [jnp.zeros(spot.shape, F32)] * 5
    )
    dp_index = dp.astype(jnp.int32)[None]

    x_mine, x_got, onehots, far_x = [], [], [], [([], []) for _ in range(1, n_dp)]
    for members in sets:
        mine, theirs, onehot_t, *far = dispatch_tagged(
            lanes, [tok_chunks[d] for d in members], width, local, spots, dp_index, n_dp,
            True, True,
        )
        onehots.append(onehot_t)
        x_mine.append(mine)
        x_got.append(swap(theirs))
        for j in range(1, n_dp):
            far_x[j - 1][0].append(dp_shift(far[2 * (j - 1)], j))
            far_x[j - 1][1].append(dp_shift_across(far[2 * (j - 1) + 1], j))
    x = x_mine + x_got
    far_x = [a + b for a, b in far_x]

    fwd = []
    hs_far = [[] for _ in range(1, n_dp)]
    for s in range(local):
        slot = (me * local + s).astype(jnp.int32)[None]
        fwd.append(forward(slot, s, x, w_gate, w_up, w_down, block, width))
        for j in range(1, n_dp):
            hs_far[j - 1].append(dp_shift(fwd[s][2], j))
    near = [f[4] for f in fwd]
    got = [swap(f[5]) for f in fwd]

    def send_home(near, got, long_fwd):
        sums = [None] * len(sets)
        for i in reversed(range(len(sets))):
            sums[i] = combine(onehots[i], near + got, i, spots)

        def part(delta):
            for i, members in enumerate(sets):
                if delta in members:
                    a = members.index(delta) * rows_dev
                    return sums[i][a:a + rows_dev]

        return ring.scatter(part, long_fwd)

    layer_out = send_home(near, got, True).astype(BF)

    g_mine, g_got = [], []
    for i, members in enumerate(sets):
        mine, theirs = dispatch_plain(onehots[i], [d_chunks[d] for d in members], local, spots)
        g_mine.append(mine)
        g_got.append(swap(theirs))
    g = g_mine + g_got

    bwd = []
    act_far = [[] for _ in range(1, n_dp)]
    for s in range(local):
        bwd.append(backward(s, g, fwd[s][0], fwd[s][1], fwd[s][3], w_gate, w_up, w_down, block))
        for j in range(1, n_dp):
            act_far[j - 1].append(dp_shift(bwd[s][0], j))
    near = [b[1] for b in bwd]
    got = [swap(b[2]) for b in bwd]
    home = send_home(near, got, False)
    d_tokens = home[:, :width].astype(BF)
    tail = home[:, width:]
    d_gates = tail[:, :top] + tail[:, top:2 * top] + tail[:, 2 * top:3 * top]

    far_g = []
    piece = width // n_dp
    for j in range(1, n_dp):
        a = (j - 1) * (piece + TAG)
        mine_all, got_all = [], []
        for members in sets:
            chunks = [far_chunks[d] for d in members]
            if n_dp > 2:
                chunks = [c[:, a:a + piece + TAG] for c in chunks]
            mine, theirs = dispatch_tagged(
                lanes, chunks, piece, local, spots, dp_index, n_dp, False, False
            )
            mine_all.append(mine)
            got_all.append(swap(theirs))
        far_g.append(mine_all + got_all)

    grad_down = down_grad(dp_index, g, far_g, [[f[2] for f in fwd]] + hs_far)
    grad_gate, grad_up = in_grads(dp_index, x, far_x, [[b[0] for b in bwd]] + act_far)
    return layer_out, d_tokens, d_gates, grad_gate, grad_up, grad_down


def solution(mesh):
    in_specs = (
        P(("dp", "expert"), None),
        P(("dp", "expert"), None),
        P(("dp", "expert"), None),
        P(),
        P("expert", None, None),
        P("expert", None, None),
        P("expert", None, None),
        P(("dp", "expert"), None),
    )
    out_specs = (
        P(("dp", "expert"), None),
        P(("dp", "expert"), None),
        P(("dp", "expert"), None),
        P("expert", "dp", None),
        P("expert", "dp", None),
        P("expert", None, "dp"),
    )
    return jax.shard_map(
        on_device, mesh=mesh, in_specs=in_specs, out_specs=out_specs, check_vma=False
    )
```
